512 devices in a mesh: dp: 32 (over x, y, z_hi), seq: 16 (over z_lo, core).
Axes of the slice: x: 4, y: 4, z: 16 (z_hi: 2, z_lo: 8; z = z_hi * 8 + z_lo), core: 2. Of those that a mesh axis runs over, the one named last changes fastest.
Arguments:
- tokens: bfloat16 [32, 2048, 2048], P('dp', 'seq'), may hold values from -60 to 60
- master: float32 [2048, 3072], P('dp', 'seq'), may hold values from -0.21875 to 0.21875
- moment_one: float32 [2048, 3072], P('dp', 'seq'), may hold values from -0.06 to 0.06
- moment_two: float32 [2048, 3072], P('dp', 'seq'), may hold values from 1e-05 to 0.0001
- gradient: float32 [2048, 3072], P('dp', 'seq'), may hold values from -0.6 to 0.6
Outputs:
- context: bfloat16 [32, 2048, 2048], P('dp', 'seq')
- new_master: float32 [2048, 3072], P('dp', 'seq')
The draws below stay inside these ranges and needn't reach their ends.
All inputs are finite; a program needn't handle non-finite values.
Results may differ from the reference program's by a relative error of at most 0.013.
The reference program's roundings to bfloat16 on the way count: a program that leaves them out, or rounds other values in their place, can miss the bound.
Values may be sent and summed in bfloat16 or wider, within the bound.
A program may use at most 64 MiB of HBM per device.

```python
import math
import jax
import jax.numpy as jnp
from jax import lax

D = 2048
HEADS = 16
KV_HEADS = 4
HEAD_DIM = 128
LEN = 2048
SEQS = 32
QKV = 3072


def draw_tokens(key, part):
    normal_key = jax.random.fold_in(key, 11)
    base = jnp.clip(jax.random.normal(normal_key, (SEQS, LEN, D), jnp.float32), -6.0, 6.0)
    return base.astype(jnp.bfloat16)


def level_of(key, dims, shards, low, high):
    def one(position, shards_of):
        steps = jax.random.uniform(jax.random.fold_in(jax.random.fold_in(key, 6), position), (shards_of,), jnp.float32, low / len(shards), high / len(shards))
        return jnp.repeat(jnp.exp(steps), dims[position] // shards_of).reshape((-1,) + (1,) * (len(dims) - position - 1))

    level = one(*shards[0])
    for cut in shards[1:]:
        level = level * one(*cut)
    return level


def bell_draw(rng, dims, deviation, reach, shards=(), kind=jnp.bfloat16):
    factor_of = level_of(rng, dims, shards, -0.22, 0.18) if shards else 1.0
    values = jax.random.normal(rng, dims, jnp.float32) * deviation * factor_of
    return jnp.minimum(jnp.maximum(values, -reach), reach).astype(kind)


def setup_inputs(seed: int = 0) -> dict:
    streams_of = jax.random.split(jax.random.key(seed), 6)
    return {
        "tokens": draw_tokens(jax.random.fold_in(streams_of[5], 71), 0),
        "master": bell_draw(streams_of[1], (D, QKV), (D // 3) ** -0.5, 0.21875, ((0, 32), (1, 16)), jnp.float32),
        "moment_one": bell_draw(streams_of[2], (D, QKV), 0.01, 0.06, ((0, 32), (1, 16)), jnp.float32),
        "moment_two": jnp.clip(jnp.exp(math.log(0.0001) - 2.3025851 * jax.random.uniform(streams_of[3], (D, QKV), jnp.float32) ** level_of(streams_of[3], (D, QKV), ((0, 32), (1, 16)), -0.2, 0.2)), 9.999999747378752e-06, 0.0001),
        "gradient": bell_draw(streams_of[4], (D, QKV), 0.1, 0.6, ((0, 32), (1, 16)), jnp.float32),
    }


beta_one = 0.9
beta_two = 0.999
learn_rate = 0.005
decay_rate = 0.1
adam_eps = 1e-08
rope_theta = 500000.0
correct_one = 1.0 - math.exp(1000.0 * math.log(beta_one))
correct_two = 1.0 - math.exp(1000.0 * math.log(beta_two))

def adam_step(master, moment_one, moment_two, gradient):
    first = beta_one * moment_one + (1.0 - beta_one) * gradient
    second = beta_two * moment_two + (1.0 - beta_two) * gradient * gradient
    update = first / correct_one / (jnp.sqrt(second / correct_two) + adam_eps)
    return master - learn_rate * (update + decay_rate * master)

def rotate_pairs(heads_in, positions):
    half_width = heads_in.shape[-1] // 2
    frequency = rope_theta ** (-(jnp.arange(half_width).astype(jnp.float32) * 2.0) / heads_in.shape[-1])
    angles = positions[:, None] * frequency[None, :]
    cosine = jnp.cos(angles)[:, None, :]
    sine = jnp.sin(angles)[:, None, :]
    lower_half = heads_in[..., :half_width]
    upper_half = heads_in[..., half_width:]
    return jnp.concatenate([lower_half * cosine - upper_half * sine, upper_half * cosine + lower_half * sine], axis=-1)

def split_heads(projected, positions):
    row_count = projected.shape[0]
    query_width = HEADS * HEAD_DIM
    key_width = KV_HEADS * HEAD_DIM
    queries = projected[:, :query_width].reshape(row_count, HEADS, HEAD_DIM)
    key_heads = projected[:, query_width:query_width + key_width].reshape(row_count, KV_HEADS, HEAD_DIM)
    value_heads = projected[:, query_width + key_width:].reshape(row_count, KV_HEADS, HEAD_DIM)
    queries = rotate_pairs(queries, positions).astype(jnp.bfloat16)
    key_heads = rotate_pairs(key_heads, positions).astype(jnp.bfloat16)
    return (queries, key_heads, value_heads.astype(jnp.bfloat16))

def reference(tokens, master, moment_one, moment_two, gradient):
    new_master = adam_step(master, moment_one, moment_two, gradient)
    weights_bf = new_master.astype(jnp.bfloat16)
    positions = jnp.arange(LEN).astype(jnp.float32)
    allowed = jnp.arange(LEN)[:, None] >= jnp.arange(LEN)[None, :]
    group_size = HEADS // KV_HEADS
    score_scale = 1.0 / math.sqrt(HEAD_DIM)

    def one_sequence(inputs):
        projected = jnp.dot(inputs, weights_bf, preferred_element_type=jnp.float32)
        queries, key_heads, value_heads = split_heads(projected, positions)

        def one_head(head):
            query_one = lax.dynamic_index_in_dim(queries, head, 1, keepdims=False)
            key_one = lax.dynamic_index_in_dim(key_heads, head // group_size, 1, keepdims=False)
            value_one = lax.dynamic_index_in_dim(value_heads, head // group_size, 1, keepdims=False)
            scores = jnp.dot(query_one, key_one.T, preferred_element_type=jnp.float32) * score_scale
            scores = jnp.where(allowed, scores, -jnp.inf)
            row_top = lax.optimization_barrier(jnp.max(scores, axis=-1, keepdims=True))
            exponent = jnp.exp(scores - row_top)
            probabilities = (exponent / lax.optimization_barrier(jnp.sum(exponent, axis=-1, keepdims=True))).astype(jnp.bfloat16)
            return jnp.dot(probabilities, value_one, preferred_element_type=jnp.float32).astype(jnp.bfloat16)
        context = lax.map(one_head, jnp.arange(HEADS))
        return jnp.transpose(context, (1, 0, 2)).reshape(LEN, HEADS * HEAD_DIM)
    return (lax.map(one_sequence, tokens), new_master)
```

```python
import functools
import math

import jax
import jax.numpy as jnp
from jax import lax
from jax.experimental import pallas as pl
from jax.experimental.pallas import tpu as pltpu
from jax.sharding import PartitionSpec as P

HEADS = 16
KV_HEADS = 4
HEAD_DIM = 128
SIDE = 4
LINE = 8
RING = 16
MESH = pl.DeviceIdType.MESH

beta_one = 0.9
beta_two = 0.999
learn_rate = 0.005
decay_rate = 0.1
adam_eps = 1e-08
rope_theta = 500000.0
correct_one = 1.0 - math.exp(1000.0 * math.log(beta_one))
correct_two = 1.0 - math.exp(1000.0 * math.log(beta_two))

SCALE = 1.0 / math.sqrt(HEAD_DIM)
BLK = 128
SUB = 64
ROWS = 128
GROUPS = ((1024, 256, True), (1280, 256, False), (0, 512, True), (512, 512, False))


def adam_step(master, moment_one, moment_two, gradient):
    first = beta_one * moment_one + (1.0 - beta_one) * gradient
    second = beta_two * moment_two + (1.0 - beta_two) * gradient * gradient
    update = first / correct_one / (jnp.sqrt(second / correct_two) + adam_eps)
    return master - learn_rate * (update + decay_rate * master)


def kernel(
    tokens, shard, cos, sin, out,
    other, blk, W, tok, kv, q, acc, top, total, ctx,
    misc, zsend, zrecv, s1send, s1recv, s2send, s2recv, kvsend, kvrecv,
):
    dp, seq = lax.axis_index("dp"), lax.axis_index("seq")
    zh = lax.rem(dp, 2)
    xy = lax.div(dp, 2)
    x, y = lax.div(xy, SIDE), lax.rem(xy, SIDE)
    c = lax.rem(seq, 2)
    zl = lax.div(seq, 2)
    z = zh * LINE + zl

    def at(xx, yy, zz, cc):
        return {
            "dp": (xx * SIDE + yy) * 2 + lax.div(zz, LINE),
            "seq": lax.rem(zz, LINE) * 2 + cc,
        }

    def xat(d):
        return lax.rem(x + (SIDE + d) % SIDE, SIDE)

    def yat(d):
        return lax.rem(y + (SIDE + d) % SIDE, SIDE)

    partner = at(x, y, z, 1 - c)

    barrier = pltpu.get_barrier_semaphore()

    def greet(target):
        pl.semaphore_signal(barrier, inc=1, device_id=target, device_id_type=MESH)

    greet(partner)
    for d in range(1, SIDE):
        greet(at(xat(d), y, z, c))
        greet(at(x, yat(d), z, c))

    def greet_z(d, carry):
        greet(at(x, y, lax.rem(z + d, RING), c))
        return carry

    lax.fori_loop(1, RING, greet_z, 0)
    mine = pl.ds(pl.multiple_of(c * 128, 128), 128)
    theirs = pl.ds(pl.multiple_of((1 - c) * 128, 128), 128)
    tok_local = pltpu.make_async_copy(tokens, tok.at[mine], misc.at[0])
    tok_local.start()
    pl.semaphore_wait(barrier, 1 + 2 * (SIDE - 1) + RING - 1)

    def remote(src, dst, send, recv, target):
        return pltpu.make_async_remote_copy(
            src_ref=src, dst_ref=dst, send_sem=send, recv_sem=recv,
            device_id=target, device_id_type=MESH,
        )

    w_copy = remote(shard, other, misc.at[3], misc.at[4], partner)
    w_copy.start()
    tok_copy = remote(tokens, tok.at[mine], misc.at[1], misc.at[2], partner)
    tok_copy.start()
    w_copy.wait_recv()

    own_shard = shard[...].astype(jnp.float32)
    other_shard = other[...].astype(jnp.float32)
    low = jnp.where(c == 0, own_shard, other_shard)
    high = jnp.where(c == 0, other_shard, own_shard)
    blk[0] = low[:, :128].astype(jnp.bfloat16)
    blk[1] = jnp.concatenate([low[:, 128:], high[:, :64]], axis=1).astype(jnp.bfloat16)
    blk[2] = high[:, 64:].astype(jnp.bfloat16)

    def place(zhalf, column):
        rows = pl.ds(pl.multiple_of(xy * ROWS + zhalf * SUB, SUB), SUB)
        return W.at[rows, pl.ds(pl.multiple_of(column, BLK), BLK)]

    def spread(j, keys_or_values):
        b = zl * 3 + j
        past = b - HEADS
        if keys_or_values:
            local = 8 + lax.div(past, KV_HEADS) * 2 + lax.rem(past, 2)
            wanted = (b >= HEADS) & (lax.rem(lax.div(past, 2), 2) == c)
        else:
            local = lax.rem(b, 8)
            wanted = (b < HEADS) & (lax.div(b, 8) == c)

        @pl.when(wanted)
        def _():
            where = place(zh, local * BLK)
            sem = zrecv.at[local * 2 + zh]

            def one(d, carry):
                remote(
                    blk.at[j], where, zsend.at[j], sem, at(x, y, lax.rem(z + d, RING), c)
                ).start()
                return carry

            lax.fori_loop(1, RING, one, 0)
            pltpu.make_async_copy(blk.at[j], where, sem).start()

    def spread_done(j):
        b = zl * 3 + j
        past = b - HEADS
        wanted = ((b < HEADS) & (lax.div(b, 8) == c)) | (
            (b >= HEADS) & (lax.rem(lax.div(past, 2), 2) == c)
        )

        @pl.when(wanted)
        def _():
            ref = W.at[pl.ds(0, SUB * (RING - 1)), pl.ds(0, BLK)]
            pltpu.make_async_copy(ref, ref, zsend.at[j]).wait()

    def landed(first, count):
        for local in range(first, first + count):
            for half in range(2):
                ref = place(half, local * BLK)
                pltpu.make_async_copy(ref, ref, zrecv.at[local * 2 + half]).wait()

    def piece(g, xx, yy):
        first, width, _ = GROUPS[g]
        rows = pl.ds(pl.multiple_of((xx * SIDE + yy) * ROWS, ROWS), ROWS)
        return W.at[rows, pl.ds(first, width)]

    def stage_one(g):
        ref = piece(g, x, y)
        for d in range(1, SIDE):
            target = at(xat(d), y, z, c) if GROUPS[g][2] else at(x, yat(d), z, c)
            remote(ref, ref, s1send.at[g], s1recv.at[g * 3 + d - 1], target).start()

    def stage_two(g, d):
        ref = piece(g, xat(-d), y) if GROUPS[g][2] else piece(g, x, yat(-d))
        if d:
            pltpu.make_async_copy(ref, ref, s1recv.at[g * 3 + d - 1]).wait()
        for e in range(1, SIDE):
            target = at(x, yat(e), z, c) if GROUPS[g][2] else at(xat(e), y, z, c)
            remote(ref, ref, s2send.at[g], s2recv.at[g * 12 + d * 3 + e - 1], target).start()

    def gathered(g):
        for d in range(SIDE):
            for e in range(1, SIDE):
                if GROUPS[g][2]:
                    ref = piece(g, xat(-d), yat(-e))
                else:
                    ref = piece(g, xat(-e), yat(-d))
                pltpu.make_async_copy(ref, ref, s2recv.at[g * 12 + d * 3 + e - 1]).wait()

    def planes_done(g):
        first, width, _ = GROUPS[g]
        ref = W.at[pl.ds(0, 3 * ROWS), pl.ds(first, width)]
        pltpu.make_async_copy(ref, ref, s1send.at[g]).wait()
        ref = W.at[pl.ds(0, 12 * ROWS), pl.ds(first, width)]
        pltpu.make_async_copy(ref, ref, s2send.at[g]).wait()

    def rotated(value):
        return value * cos[...] + pltpu.roll(value, 64, 1) * sin[...]

    for j in range(3):
        spread(j, True)
    landed(8, 2)
    stage_one(0)
    landed(10, 2)
    stage_one(1)
    for j in range(3):
        spread(j, False)
    stage_two(0, 0)
    stage_two(1, 0)
    for d in range(1, SIDE):
        stage_two(0, d)
        stage_two(1, d)
    landed(0, 4)
    stage_one(2)
    landed(4, 4)
    stage_one(3)
    stage_two(2, 0)
    stage_two(3, 0)
    tok_local.wait()
    tok_copy.wait_recv()

    gathered(0)
    keys = jnp.dot(tok[...], W[:, 1024:1280], preferred_element_type=jnp.float32)
    for h in range(2):
        kv[zl, h] = rotated(keys[:, h * 128 : (h + 1) * 128]).astype(jnp.bfloat16)
    gathered(1)
    values = jnp.dot(tok[...], W[:, 1280:1536], preferred_element_type=jnp.float32)
    for h in range(2):
        kv[zl, 2 + h] = values[:, h * 128 : (h + 1) * 128].astype(jnp.bfloat16)

    def kv_copy(s):
        ref = kv.at[zl - s]
        return remote(ref, ref, kvsend.at[s], kvrecv.at[s], at(x, y, z + 1, c))

    @pl.when(zl < LINE - 1)
    def _():
        kv_copy(0).start()

    for d in range(1, SIDE):
        stage_two(2, d)
        stage_two(3, d)

    def arrive(s):
        @pl.when(zl > s)
        def _():
            ref = kv.at[zl - 1 - s]
            pltpu.make_async_copy(ref, ref, kvrecv.at[s]).wait()

        if s + 1 < LINE - 1:

            @pl.when((zl > s) & (zl < LINE - 1))
            def _():
                kv_copy(s + 1).start()

    def project_queries():
        def pair(i, carry):
            cols = pl.ds(pl.multiple_of(i * 256, 256), 256)
            two = jnp.dot(tok[...], W[:, cols], preferred_element_type=jnp.float32)
            q[i * 2] = rotated(two[:, :128]).astype(jnp.bfloat16)
            q[i * 2 + 1] = rotated(two[:, 128:]).astype(jnp.bfloat16)
            return carry

        lax.fori_loop(0, 4, pair, 0)

    NT = (((1,), (1,)), ((), ()))

    def diagonal():
        keep = lax.broadcasted_iota(jnp.int32, (256, 256), 0) >= lax.broadcasted_iota(
            jnp.int32, (256, 256), 1
        )

        def group(i, carry):
            key, value = kv[zl, i], kv[zl, 2 + i]
            for j in range(4):
                h = i * 4 + j
                s = lax.dot_general(q[h], key, NT, preferred_element_type=jnp.float32)
                s = jnp.where(keep, s, -jnp.inf)
                m = jnp.max(s, axis=-1, keepdims=True)
                p = jnp.exp((s - m) * SCALE)
                top[h] = m
                total[h] = jnp.sum(p, axis=-1, keepdims=True)
                acc[h] = jnp.dot(
                    p.astype(jnp.bfloat16), value, preferred_element_type=jnp.float32
                )
            return carry

        lax.fori_loop(0, 2, group, 0)

    def attend(step):
        @pl.when(zl > step)
        def _():
            slot = zl - 1 - step

            def group(i, carry):
                key, value = kv[slot, i], kv[slot, 2 + i]
                for j in range(4):
                    h = i * 4 + j
                    s = lax.dot_general(q[h], key, NT, preferred_element_type=jnp.float32)
                    old = top[h]
                    m = jnp.maximum(old, jnp.max(s, axis=-1, keepdims=True))
                    p = jnp.exp((s - m) * SCALE)
                    shrink = jnp.exp((old - m) * SCALE)
                    top[h] = m
                    total[h] = total[h] * shrink + jnp.sum(p, axis=-1, keepdims=True)
                    acc[h] = acc[h] * shrink + jnp.dot(
                        p.astype(jnp.bfloat16), value, preferred_element_type=jnp.float32
                    )
                return carry

            lax.fori_loop(0, 2, group, 0)

    for s in range(4):
        arrive(s)
    gathered(2)
    gathered(3)
    project_queries()
    diagonal()
    attend(0)
    arrive(4)
    attend(1)
    attend(2)
    arrive(5)
    attend(3)
    attend(4)
    arrive(6)
    attend(5)
    attend(6)

    for h in range(8):
        value = (acc[h] / total[h]).astype(jnp.bfloat16)
        ctx[:, h * 128 : (h + 1) * 128] = value
    columns = pl.ds(pl.multiple_of(c * 1024, 1024), 1024)
    out_copy = remote(
        ctx.at[theirs], out.at[:, columns], misc.at[6], misc.at[7], partner
    )
    out_copy.start()
    out_local = pltpu.make_async_copy(ctx.at[mine], out.at[:, columns], misc.at[5])
    out_local.start()

    w_copy.wait_send()
    tok_copy.wait_send()
    for j in range(3):
        spread_done(j)
    for g in range(4):
        planes_done(g)
    for s in range(LINE - 1):

        @pl.when((zl >= s) & (zl < LINE - 1))
        def _(s=s):
            kv_copy(s).wait_send()

    out_local.wait()
    out_copy.wait()


def shards(tokens, master, moment_one, moment_two, gradient):
    new_master = adam_step(master, moment_one, moment_two, gradient)
    weights = new_master.astype(jnp.bfloat16)
    half = HEAD_DIM // 2
    frequency = rope_theta ** (-(jnp.arange(half).astype(jnp.float32) * 2.0) / HEAD_DIM)
    chip = lax.div(lax.axis_index("seq"), 2)
    positions = (chip * 256 + jnp.arange(256)).astype(jnp.float32)
    angles = positions[:, None] * frequency[None, :]
    cosine, sine = jnp.cos(angles), jnp.sin(angles)
    cos = jnp.concatenate([cosine, cosine], axis=1)
    sin = jnp.concatenate([-sine, sine], axis=1)
    vmem = pl.BlockSpec(memory_space=pltpu.VMEM)
    anywhere = pl.BlockSpec(memory_space=pl.ANY)
    bf16, f32 = jnp.bfloat16, jnp.float32
    dma = pltpu.SemaphoreType.DMA
    context = pl.pallas_call(
        kernel,
        name="gather_attend",
        out_shape=jax.ShapeDtypeStruct((128, 2048), bf16),
        in_specs=[anywhere, vmem, vmem, vmem],
        out_specs=anywhere,
        scratch_shapes=[
            pltpu.VMEM((64, 192), bf16),
            pltpu.VMEM((3, 64, 128), bf16),
            pltpu.VMEM((2048, 1536), bf16),
            pltpu.VMEM((256, 2048), bf16),
            pltpu.VMEM((LINE, 4, 256, 128), bf16),
            pltpu.VMEM((8, 256, 128), bf16),
            pltpu.VMEM((8, 256, 128), f32),
            pltpu.VMEM((8, 256, 1), f32),
            pltpu.VMEM((8, 256, 1), f32),
            pltpu.VMEM((256, 1024), bf16),
            dma((8,)), dma((3,)), dma((24,)), dma((4,)), dma((12,)), dma((4,)), dma((48,)),
            dma((7,)), dma((7,)),
        ],
        compiler_params=pltpu.CompilerParams(
            collective_id=0, has_side_effects=True, vmem_limit_bytes=48 * 1024 * 1024
        ),
    )(tokens[0], weights, cos, sin)
    return context[None], new_master


def solution(mesh):
    placed = (P("dp", "seq", None), P("dp", "seq"), P("dp", "seq"), P("dp", "seq"), P("dp", "seq"))
    return jax.shard_map(
        shards,
        mesh=mesh,
        in_specs=placed,
        out_specs=(P("dp", "seq", None), P("dp", "seq")),
        check_vma=False,
    )
```

```python
import functools
import math

import jax
import jax.numpy as jnp
from jax import lax
from jax.experimental import pallas as pl
from jax.experimental.pallas import tpu as pltpu
from jax.sharding import PartitionSpec as P

HEADS = 16
KV_HEADS = 4
HEAD_DIM = 128
SIDE = 4
LINE = 8
RING = 16
MESH = pl.DeviceIdType.MESH

beta_one = 0.9
beta_two = 0.999
learn_rate = 0.005
decay_rate = 0.1
adam_eps = 1e-08
rope_theta = 500000.0
correct_one = 1.0 - math.exp(1000.0 * math.log(beta_one))
correct_two = 1.0 - math.exp(1000.0 * math.log(beta_two))

SCALE = 1.0 / math.sqrt(HEAD_DIM)
BLK = 128
SUB = 64
ROWS = 128
GROUPS = (
    (1024, 128, True), (1152, 128, False), (1280, 128, True), (1408, 128, False),
    (0, 256, True), (512, 256, False), (256, 256, True), (768, 256, False),
)
COARSE = (8, 4, 12)
FINE = (1, 15, 2)
POWER = SCALE / math.log(2.0)


def adam_step(master, moment_one, moment_two, gradient):
    first = beta_one * moment_one + (1.0 - beta_one) * gradient
    second = beta_two * moment_two + (1.0 - beta_two) * gradient * gradient
    update = first / correct_one / (jnp.sqrt(second / correct_two) + adam_eps)
    return master - learn_rate * (update + decay_rate * master)


def kernel(
    tokens, shard, cos, sin, out,
    other, blk, W, tok, keys, values, q, acc, top, total, ctx,
    misc, zsend, zpass, zrecv, s1send, s1recv, s2send, s2recv, kvsend, kvrecv,
):
    dp, seq = lax.axis_index("dp"), lax.axis_index("seq")
    zh = lax.rem(dp, 2)
    xy = lax.div(dp, 2)
    x, y = lax.div(xy, SIDE), lax.rem(xy, SIDE)
    c = lax.rem(seq, 2)
    zl = lax.div(seq, 2)
    z = zh * LINE + zl

    def at(xx, yy, zz, cc):
        return {
            "dp": (xx * SIDE + yy) * 2 + lax.div(zz, LINE),
            "seq": lax.rem(zz, LINE) * 2 + cc,
        }

    def xat(d):
        return lax.rem(x + (SIDE + d) % SIDE, SIDE)

    def yat(d):
        return lax.rem(y + (SIDE + d) % SIDE, SIDE)

    partner = at(x, y, z, 1 - c)

    barrier = pltpu.get_barrier_semaphore()

    def greet(target):
        pl.semaphore_signal(barrier, inc=1, device_id=target, device_id_type=MESH)

    greet(partner)
    for d in range(1, SIDE):
        greet(at(xat(d), y, z, c))
        greet(at(x, yat(d), z, c))

    def greet_z(d, carry):
        greet(at(x, y, lax.rem(z + d, RING), c))
        return carry

    lax.fori_loop(1, RING, greet_z, 0)
    mine = pl.ds(pl.multiple_of(c * 128, 128), 128)
    theirs = pl.ds(pl.multiple_of((1 - c) * 128, 128), 128)
    tok_local = pltpu.make_async_copy(tokens, tok.at[mine], misc.at[0])
    tok_local.start()
    pl.semaphore_wait(barrier, 1 + 2 * (SIDE - 1) + RING - 1)

    def remote(src, dst, send, recv, target):
        return pltpu.make_async_remote_copy(
            src_ref=src, dst_ref=dst, send_sem=send, recv_sem=recv,
            device_id=target, device_id_type=MESH,
        )

    w_copy = remote(shard, other, misc.at[3], misc.at[4], partner)
    w_copy.start()
    tok_copy = remote(tokens, tok.at[mine], misc.at[1], misc.at[2], partner)
    tok_copy.start()
    w_copy.wait_recv()

    own_shard = shard[...].astype(jnp.float32)
    other_shard = other[...].astype(jnp.float32)
    low = jnp.where(c == 0, own_shard, other_shard)
    high = jnp.where(c == 0, other_shard, own_shard)
    blk[0] = low[:, :128].astype(jnp.bfloat16)
    blk[1] = jnp.concatenate([low[:, 128:], high[:, :64]], axis=1).astype(jnp.bfloat16)
    blk[2] = high[:, 64:].astype(jnp.bfloat16)

    def place(zhalf, column):
        rows = pl.ds(pl.multiple_of(xy * ROWS + zhalf * SUB, SUB), SUB)
        return W.at[rows, pl.ds(pl.multiple_of(column, BLK), BLK)]

    def block_of(line, j, keys_or_values):
        b = line * 3 + j
        past = b - HEADS
        if keys_or_values:
            local = 8 + lax.div(past, KV_HEADS) * 2 + lax.rem(past, 2)
            return local, (b >= HEADS) & (lax.rem(lax.div(past, 2), 2) == c)
        return lax.rem(b, 8), (b < HEADS) & (lax.div(b, 8) == c)

    def z_send(src, where, send, recv, steps):
        for d in steps:
            remote(src, where, send, recv, at(x, y, lax.rem(z + d, RING), c)).start()

    def spread(kind):
        for j in range(3):
            local, wanted = block_of(zl, j, kind)

            @pl.when(wanted)
            def _(j=j, local=local):
                where = place(zh, local * BLK)
                sem = zrecv.at[local * 2 + zh]
                z_send(blk.at[j], where, zsend.at[j], sem, COARSE + FINE)
                pltpu.make_async_copy(blk.at[j], where, sem).start()

    def pass_on(kind):
        for i, d in enumerate(COARSE):
            source = lax.rem(z + RING - d, RING)
            half = lax.div(source, LINE)
            for j in range(3):
                local, wanted = block_of(lax.rem(source, LINE), j, kind)

                @pl.when(wanted)
                def _(i=i, j=j, local=local, half=half):
                    where = place(half, local * BLK)
                    sem = zrecv.at[local * 2 + half]
                    pltpu.make_async_copy(where, where, sem).wait()
                    z_send(where, where, zpass.at[i * 3 + j], sem, FINE)

    def spread_done():
        for kind in (True, False):
            for j in range(3):
                _, wanted = block_of(zl, j, kind)

                @pl.when(wanted)
                def _(j=j):
                    ref = W.at[pl.ds(0, SUB * 6), pl.ds(0, BLK)]
                    pltpu.make_async_copy(ref, ref, zsend.at[j]).wait()

                for i, d in enumerate(COARSE):
                    _, passed = block_of(lax.rem(z + RING - d, LINE), j, kind)

                    @pl.when(passed)
                    def _(i=i, j=j):
                        ref = W.at[pl.ds(0, SUB * 3), pl.ds(0, BLK)]
                        pltpu.make_async_copy(ref, ref, zpass.at[i * 3 + j]).wait()

    def landed(first, count):
        for local in range(first, first + count):
            if local < 8:
                b = c * 8 + local
            elif local < 10:
                b = HEADS + c * 2 + local - 8
            else:
                b = HEADS + KV_HEADS + c * 2 + local - 10
            for half in range(2):
                steps = lax.rem(z + RING - (lax.div(b, 3) + half * LINE), RING)

                @pl.when((lax.rem(steps, 4) != 0) | (steps == 0))
                def _(local=local, half=half):
                    ref = place(half, local * BLK)
                    pltpu.make_async_copy(ref, ref, zrecv.at[local * 2 + half]).wait()

    def piece(g, xx, yy):
        first, width, _ = GROUPS[g]
        rows = pl.ds(pl.multiple_of((xx * SIDE + yy) * ROWS, ROWS), ROWS)
        return W.at[rows, pl.ds(first, width)]

    def stage_one(g):
        ref = piece(g, x, y)
        for d in range(1, SIDE):
            target = at(xat(d), y, z, c) if GROUPS[g][2] else at(x, yat(d), z, c)
            remote(ref, ref, s1send.at[g], s1recv.at[g * 3 + d - 1], target).start()

    def stage_two(g, d):
        ref = piece(g, xat(-d), y) if GROUPS[g][2] else piece(g, x, yat(-d))
        if d:
            pltpu.make_async_copy(ref, ref, s1recv.at[g * 3 + d - 1]).wait()
        for e in range(1, SIDE):
            target = at(x, yat(e), z, c) if GROUPS[g][2] else at(xat(e), y, z, c)
            remote(ref, ref, s2send.at[g], s2recv.at[g * 12 + d * 3 + e - 1], target).start()

    def gathered(g):
        for d in range(SIDE):
            for e in range(1, SIDE):
                if GROUPS[g][2]:
                    ref = piece(g, xat(-d), yat(-e))
                else:
                    ref = piece(g, xat(-e), yat(-d))
                pltpu.make_async_copy(ref, ref, s2recv.at[g * 12 + d * 3 + e - 1]).wait()

    def planes_done(g):
        first, width, _ = GROUPS[g]
        ref = W.at[pl.ds(0, 3 * ROWS), pl.ds(first, width)]
        pltpu.make_async_copy(ref, ref, s1send.at[g]).wait()
        ref = W.at[pl.ds(0, 12 * ROWS), pl.ds(first, width)]
        pltpu.make_async_copy(ref, ref, s2send.at[g]).wait()

    def rotated(value):
        return value * cos[...] + pltpu.roll(value, 64, 1) * sin[...]

    def kv_copy(kind, s):
        ref = (values if kind else keys).at[zl - s]
        sem = kind * (LINE - 1) + s
        return remote(ref, ref, kvsend.at[sem], kvrecv.at[sem], at(x, y, z + 1, c))

    def send_own(kind):
        @pl.when(zl < LINE - 1)
        def _():
            kv_copy(kind, 0).start()

    def arrive(kind, s):
        @pl.when(zl > s)
        def _():
            ref = (values if kind else keys).at[zl - 1 - s]
            pltpu.make_async_copy(ref, ref, kvrecv.at[kind * (LINE - 1) + s]).wait()

        if s + 1 < LINE - 1:

            @pl.when((zl > s) & (zl < LINE - 1))
            def _():
                kv_copy(kind, s + 1).start()

    def project_queries(offset):
        def pair(i, carry):
            cols = pl.ds(pl.multiple_of(i * 512 + offset * 128, 256), 256)
            two = jnp.dot(tok[...], W[:, cols], preferred_element_type=jnp.float32)
            for j in range(2):
                one = rotated(two[:, j * 128 : (j + 1) * 128])
                q[i * 4 + offset + j] = one.T.astype(jnp.bfloat16)
            return carry

        lax.fori_loop(0, 2, pair, 0)

    def attend(slot, offset, masked):
        def group(i, carry):
            key, value = keys[slot, i], values[slot, i]
            for j in range(2):
                h = i * 4 + offset + j
                s = jnp.dot(key, q[h], preferred_element_type=jnp.float32)
                if masked:
                    row = lax.broadcasted_iota(jnp.int32, (256, 256), 0)
                    column = lax.broadcasted_iota(jnp.int32, (256, 256), 1)
                    s = jnp.where(row <= column, s, -jnp.inf)
                    m = jnp.max(s, axis=0, keepdims=True)
                else:
                    old = top[h]
                    m = jnp.maximum(old, jnp.max(s, axis=0, keepdims=True))
                p = jnp.exp2((s - m) * POWER)
                mass = jnp.sum(p, axis=0, keepdims=True)
                part = jnp.dot(value, p.astype(jnp.bfloat16), preferred_element_type=jnp.float32)
                top[h] = m
                if masked:
                    total[h] = mass
                    acc[h] = part
                else:
                    shrink = jnp.exp2((old - m) * POWER)
                    total[h] = total[h] * shrink + mass
                    acc[h] = acc[h] * shrink + part
            return carry

        lax.fori_loop(0, 2, group, 0)

    def attend_steps(offset, steps):
        for s in steps:

            @pl.when(zl > s)
            def _(s=s):
                attend(zl - 1 - s, offset, False)

    spread(True)
    pass_on(True)
    spread(False)
    landed(8, 1)
    stage_one(0)
    landed(9, 1)
    stage_one(1)
    landed(10, 1)
    stage_one(2)
    landed(11, 1)
    stage_one(3)
    stage_two(0, 0)
    stage_two(1, 0)
    for d in range(1, SIDE):
        stage_two(0, d)
        stage_two(1, d)
    stage_two(2, 0)
    stage_two(3, 0)
    for d in range(1, SIDE):
        stage_two(2, d)
        stage_two(3, d)
    pass_on(False)
    tok_local.wait()
    tok_copy.wait_recv()
    gathered(0)
    gathered(1)
    two = jnp.dot(tok[...], W[:, 1024:1280], preferred_element_type=jnp.float32)
    for h in range(2):
        keys[zl, h] = rotated(two[:, h * 128 : (h + 1) * 128]).astype(jnp.bfloat16)
    send_own(0)
    landed(0, 2)
    stage_one(4)
    landed(4, 2)
    stage_one(5)
    stage_two(4, 0)
    stage_two(5, 0)
    gathered(2)
    gathered(3)
    two = jnp.dot(tok[...], W[:, 1280:1536], preferred_element_type=jnp.float32)
    for h in range(2):
        values[zl, h] = two[:, h * 128 : (h + 1) * 128].T.astype(jnp.bfloat16)
    send_own(1)
    landed(2, 2)
    stage_one(6)
    landed(6, 2)
    stage_one(7)
    arrive(0, 0)
    arrive(1, 0)
    for d in range(1, SIDE):
        stage_two(4, d)
        stage_two(5, d)
    stage_two(6, 0)
    stage_two(7, 0)
    arrive(0, 1)
    arrive(1, 1)
    for d in range(1, SIDE):
        stage_two(6, d)
        stage_two(7, d)
    arrive(0, 2)
    arrive(1, 2)
    arrive(0, 3)
    gathered(4)
    gathered(5)
    arrive(1, 3)
    project_queries(0)
    attend(zl, 0, True)
    attend_steps(0, (0, 1))
    arrive(0, 4)
    attend_steps(0, (2, 3))
    arrive(1, 4)
    attend_steps(0, (4,))
    arrive(0, 5)
    arrive(1, 5)
    gathered(6)
    gathered(7)
    project_queries(2)
    attend(zl, 2, True)
    attend_steps(2, (0, 1, 2, 3))
    arrive(0, 6)
    attend_steps(2, (4, 5))
    attend_steps(0, (5,))
    arrive(1, 6)
    attend_steps(2, (6,))
    attend_steps(0, (6,))

    for h in range(8):
        value = acc[h] * (1.0 / total[h])
        ctx[:, h * 128 : (h + 1) * 128] = value.T.astype(jnp.bfloat16)
    columns = pl.ds(pl.multiple_of(c * 1024, 1024), 1024)
    out_copy = remote(
        ctx.at[theirs], out.at[:, columns], misc.at[6], misc.at[7], partner
    )
    out_copy.start()
    out_local = pltpu.make_async_copy(ctx.at[mine], out.at[:, columns], misc.at[5])
    out_local.start()

    w_copy.wait_send()
    tok_copy.wait_send()
    spread_done()
    for g in range(len(GROUPS)):
        planes_done(g)
    for kind in range(2):
        for s in range(LINE - 1):

            @pl.when((zl >= s) & (zl < LINE - 1))
            def _(kind=kind, s=s):
                kv_copy(kind, s).wait_send()

    out_local.wait()
    out_copy.wait()


def shards(tokens, master, moment_one, moment_two, gradient):
    new_master = adam_step(master, moment_one, moment_two, gradient)
    weights = new_master.astype(jnp.bfloat16)
    half = HEAD_DIM // 2
    frequency = rope_theta ** (-(jnp.arange(half).astype(jnp.float32) * 2.0) / HEAD_DIM)
    chip = lax.div(lax.axis_index("seq"), 2)
    positions = (chip * 256 + jnp.arange(256)).astype(jnp.float32)
    angles = positions[:, None] * frequency[None, :]
    cosine, sine = jnp.cos(angles), jnp.sin(angles)
    cos = jnp.concatenate([cosine, cosine], axis=1)
    sin = jnp.concatenate([-sine, sine], axis=1)
    vmem = pl.BlockSpec(memory_space=pltpu.VMEM)
    anywhere = pl.BlockSpec(memory_space=pl.ANY)
    bf16, f32 = jnp.bfloat16, jnp.float32
    dma = pltpu.SemaphoreType.DMA
    context = pl.pallas_call(
        kernel,
        name="gather_attend",
        out_shape=jax.ShapeDtypeStruct((128, 2048), bf16),
        in_specs=[anywhere, vmem, vmem, vmem],
        out_specs=anywhere,
        scratch_shapes=[
            pltpu.VMEM((64, 192), bf16),
            pltpu.VMEM((3, 64, 128), bf16),
            pltpu.VMEM((2048, 1536), bf16),
            pltpu.VMEM((256, 2048), bf16),
            pltpu.VMEM((LINE, 2, 256, 128), bf16),
            pltpu.VMEM((LINE, 2, 128, 256), bf16),
            pltpu.VMEM((8, 128, 256), bf16),
            pltpu.VMEM((8, 128, 256), f32),
            pltpu.VMEM((8, 1, 256), f32),
            pltpu.VMEM((8, 1, 256), f32),
            pltpu.VMEM((256, 1024), bf16),
            dma((8,)), dma((3,)), dma((9,)), dma((24,)), dma((8,)), dma((24,)), dma((8,)),
            dma((96,)), dma((14,)), dma((14,)),
        ],
        compiler_params=pltpu.CompilerParams(
            collective_id=0, has_side_effects=True, vmem_limit_bytes=48 * 1024 * 1024
        ),
    )(tokens[0], weights, cos, sin)
    return context[None], new_master


def solution(mesh):
    placed = (P("dp", "seq", None), P("dp", "seq"), P("dp", "seq"), P("dp", "seq"), P("dp", "seq"))
    return jax.shard_map(
        shards,
        mesh=mesh,
        in_specs=placed,
        out_specs=(P("dp", "seq", None), P("dp", "seq")),
        check_vma=False,
    )
```

```python
import functools
import math

import jax
import jax.numpy as jnp
from jax import lax
from jax.experimental import pallas as pl
from jax.experimental.pallas import tpu as pltpu
from jax.sharding import PartitionSpec as P

HEADS = 16
KV_HEADS = 4
HEAD_DIM = 128
SIDE = 4
LINE = 8
RING = 16
MESH = pl.DeviceIdType.MESH

beta_one = 0.9
beta_two = 0.999
learn_rate = 0.005
decay_rate = 0.1
adam_eps = 1e-08
rope_theta = 500000.0
correct_one = 1.0 - math.exp(1000.0 * math.log(beta_one))
correct_two = 1.0 - math.exp(1000.0 * math.log(beta_two))

SCALE = 1.0 / math.sqrt(HEAD_DIM)
BLK = 128
SUB = 64
ROWS = 128
GROUPS = (
    (1024, 128, True), (1152, 128, False), (1280, 128, True), (1408, 128, False),
    (0, 256, True), (512, 256, False), (256, 256, True), (768, 256, False),
)
COARSE = (8, 4, 12)
FINE = (1, 15, 2)
STEPS = 5
POWER = SCALE / math.log(2.0)


def adam_step(master, moment_one, moment_two, gradient):
    first = beta_one * moment_one + (1.0 - beta_one) * gradient
    second = beta_two * moment_two + (1.0 - beta_two) * gradient * gradient
    update = first / correct_one / (jnp.sqrt(second / correct_two) + adam_eps)
    return master - learn_rate * (update + decay_rate * master)


def kernel(
    tokens, shard, cos, sin, out,
    other, blk, W, tok, prev, keys, values, q, acc, top, total, ctx,
    far_keys, far_values, misc, zsend, zpass, zrecv, s1send, s1recv, s2send, s2recv, kvsend, kvrecv, wrapsend, wraprecv,
):
    dp, seq = lax.axis_index("dp"), lax.axis_index("seq")
    zh = lax.rem(dp, 2)
    xy = lax.div(dp, 2)
    x, y = lax.div(xy, SIDE), lax.rem(xy, SIDE)
    c = lax.rem(seq, 2)
    zl = lax.div(seq, 2)
    z = zh * LINE + zl

    def at(xx, yy, zz, cc):
        return {
            "dp": (xx * SIDE + yy) * 2 + lax.div(zz, LINE),
            "seq": lax.rem(zz, LINE) * 2 + cc,
        }

    def xat(d):
        return lax.rem(x + (SIDE + d) % SIDE, SIDE)

    def yat(d):
        return lax.rem(y + (SIDE + d) % SIDE, SIDE)

    partner = at(x, y, z, 1 - c)

    barrier = pltpu.get_barrier_semaphore()

    def greet(target):
        pl.semaphore_signal(barrier, inc=1, device_id=target, device_id_type=MESH)

    greet(partner)
    for d in range(1, SIDE):
        greet(at(xat(d), y, z, c))
        greet(at(x, yat(d), z, c))

    def greet_z(d, carry):
        greet(at(x, y, lax.rem(z + d, RING), c))
        return carry

    lax.fori_loop(1, RING, greet_z, 0)
    mine = pl.ds(pl.multiple_of(c * 128, 128), 128)
    theirs = pl.ds(pl.multiple_of((1 - c) * 128, 128), 128)
    tok_local = pltpu.make_async_copy(tokens, tok.at[mine], misc.at[0])
    tok_local.start()
    pl.semaphore_wait(barrier, 1 + 2 * (SIDE - 1) + RING - 1)

    def remote(src, dst, send, recv, target):
        return pltpu.make_async_remote_copy(
            src_ref=src, dst_ref=dst, send_sem=send, recv_sem=recv,
            device_id=target, device_id_type=MESH,
        )

    w_copy = remote(shard, other, misc.at[3], misc.at[4], partner)
    w_copy.start()
    tok_copy = remote(tokens, tok.at[mine], misc.at[1], misc.at[2], partner)
    tok_copy.start()
    w_copy.wait_recv()

    own_shard = shard[...].astype(jnp.float32)
    other_shard = other[...].astype(jnp.float32)
    low = jnp.where(c == 0, own_shard, other_shard)
    high = jnp.where(c == 0, other_shard, own_shard)
    blk[0] = low[:, :128].astype(jnp.bfloat16)
    blk[1] = jnp.concatenate([low[:, 128:], high[:, :64]], axis=1).astype(jnp.bfloat16)
    blk[2] = high[:, 64:].astype(jnp.bfloat16)

    def place(zhalf, column):
        rows = pl.ds(pl.multiple_of(xy * ROWS + zhalf * SUB, SUB), SUB)
        return W.at[rows, pl.ds(pl.multiple_of(column, BLK), BLK)]

    def block_of(line, j, keys_or_values):
        b = line * 3 + j
        past = b - HEADS
        if keys_or_values:
            local = 8 + lax.div(past, KV_HEADS) * 2 + lax.rem(past, 2)
            return local, (b >= HEADS) & (lax.rem(lax.div(past, 2), 2) == c)
        return lax.rem(b, 8), (b < HEADS) & (lax.div(b, 8) == c)

    def z_send(src, where, send, recv, steps):
        for d in steps:
            remote(src, where, send, recv, at(x, y, lax.rem(z + d, RING), c)).start()

    def spread(kind):
        for j in range(3):
            local, wanted = block_of(zl, j, kind)

            @pl.when(wanted)
            def _(j=j, local=local):
                where = place(zh, local * BLK)
                sem = zrecv.at[local * 2 + zh]
                z_send(blk.at[j], where, zsend.at[j], sem, COARSE + FINE)
                pltpu.make_async_copy(blk.at[j], where, sem).start()

    def pass_on(kind):
        for i, d in enumerate(COARSE):
            source = lax.rem(z + RING - d, RING)
            half = lax.div(source, LINE)
            for j in range(3):
                local, wanted = block_of(lax.rem(source, LINE), j, kind)

                @pl.when(wanted)
                def _(i=i, j=j, local=local, half=half):
                    where = place(half, local * BLK)
                    sem = zrecv.at[local * 2 + half]
                    pltpu.make_async_copy(where, where, sem).wait()
                    z_send(where, where, zpass.at[i * 3 + j], sem, FINE)

    def spread_done():
        for kind in (True, False):
            for j in range(3):
                _, wanted = block_of(zl, j, kind)

                @pl.when(wanted)
                def _(j=j):
                    ref = W.at[pl.ds(0, SUB * 6), pl.ds(0, BLK)]
                    pltpu.make_async_copy(ref, ref, zsend.at[j]).wait()

                for i, d in enumerate(COARSE):
                    _, passed = block_of(lax.rem(z + RING - d, LINE), j, kind)

                    @pl.when(passed)
                    def _(i=i, j=j):
                        ref = W.at[pl.ds(0, SUB * 3), pl.ds(0, BLK)]
                        pltpu.make_async_copy(ref, ref, zpass.at[i * 3 + j]).wait()

    def landed(first, count):
        for local in range(first, first + count):
            if local < 8:
                b = c * 8 + local
            elif local < 10:
                b = HEADS + c * 2 + local - 8
            else:
                b = HEADS + KV_HEADS + c * 2 + local - 10
            for half in range(2):
                steps = lax.rem(z + RING - (lax.div(b, 3) + half * LINE), RING)

                @pl.when((lax.rem(steps, 4) != 0) | (steps == 0))
                def _(local=local, half=half):
                    ref = place(half, local * BLK)
                    pltpu.make_async_copy(ref, ref, zrecv.at[local * 2 + half]).wait()

    def ring(g, stage, d):
        along_x = GROUPS[g][2] == (stage == 1)

        def ref(step, first=0, count=ROWS):
            dx, dy = (-step, -d) if along_x else (-d, -step)
            rows = pl.multiple_of((xat(dx) * SIDE + yat(dy)) * ROWS + first, SUB)
            return W.at[pl.ds(rows, count), pl.ds(GROUPS[g][0], GROUPS[g][1])]

        up = at(xat(1), y, z, c) if along_x else at(x, yat(1), z, c)
        down = at(xat(-1), y, z, c) if along_x else at(x, yat(-1), z, c)
        if stage == 1:
            return ref, up, down, s1send.at[g], lambda i: s1recv.at[g * 4 + i]
        return ref, up, down, s2send.at[g], lambda i: s2recv.at[(g * 4 + d) * 4 + i]

    def begin(g, stage, d=0):
        ref, up, down, send, recv = ring(g, stage, d)
        remote(ref(0), ref(0), send, recv(0), up).start()
        remote(ref(0), ref(0), send, recv(1), down).start()

    def hand_on(g, stage, d=0):
        ref, up, down, send, recv = ring(g, stage, d)
        pltpu.make_async_copy(ref(1), ref(1), recv(0)).wait()
        half = ref(1, 0, SUB)
        remote(half, half, send, recv(2), up).start()
        pltpu.make_async_copy(ref(3), ref(3), recv(1)).wait()
        half = ref(3, SUB, SUB)
        remote(half, half, send, recv(3), down).start()

    def complete(g, stage, d=0):
        ref, _, _, _, recv = ring(g, stage, d)
        for i in range(2):
            half = ref(2, i * SUB, SUB)
            pltpu.make_async_copy(half, half, recv(2 + i)).wait()

    def first_own(*groups):
        for g in groups:
            begin(g, 1)

    def second_own(*groups):
        for g in groups:
            begin(g, 2, 0)

    def first_near(*groups):
        for g in groups:
            hand_on(g, 1)
            begin(g, 2, 1)
            begin(g, 2, 3)

    def first_far(*groups):
        for g in groups:
            complete(g, 1)
            begin(g, 2, 2)

    def second_near(d, *groups):
        for g in groups:
            hand_on(g, 2, d)

    def gathered(*groups):
        for g in groups:
            for d in (0, 1, 3, 2):
                complete(g, 2, d)

    def planes_done(g):
        first, width, _ = GROUPS[g]
        ref = W.at[pl.ds(0, 3 * ROWS), pl.ds(first, width)]
        pltpu.make_async_copy(ref, ref, s1send.at[g]).wait()
        ref = W.at[pl.ds(0, 12 * ROWS), pl.ds(first, width)]
        pltpu.make_async_copy(ref, ref, s2send.at[g]).wait()

    def rotated(value, first):
        rows = slice(first, first + 256)
        return value * cos[rows] + pltpu.roll(value, 64, 1) * sin[rows]

    def kv_copy(kind, s):
        ref = (values if kind else keys).at[zl - 1 - s]
        sem = kind * STEPS + s
        return remote(ref, ref, kvsend.at[sem], kvrecv.at[sem], at(x, y, z + 1, c))

    def wrap_out(kind):
        return remote(
            (values if kind else keys).at[0], far_values if kind else far_keys,
            wrapsend.at[kind], wraprecv.at[kind], at(x, y, lax.rem(z + 9, RING), c),
        )

    def wrap_relay(kind):
        return remote(
            far_values if kind else far_keys, (values if kind else keys).at[0],
            wrapsend.at[2 + kind], wraprecv.at[2 + kind], at(x, y, lax.rem(z + RING - 2, RING), c),
        )

    def relay(kind):
        @pl.when(zl == 1)
        def _():
            ref = far_values if kind else far_keys
            pltpu.make_async_copy(ref, ref, wraprecv.at[kind]).wait()
            wrap_relay(kind).start()

    def wrapped(kind):
        @pl.when(zl == LINE - 1)
        def _():
            ref = (values if kind else keys).at[0]
            pltpu.make_async_copy(ref, ref, wraprecv.at[2 + kind]).wait()

    def attend_wrapped(offset):
        @pl.when(zl == LINE - 1)
        def _():
            attend(0, offset, False)

    def wrap_done():
        for kind in range(2):

            @pl.when(zl == 0)
            def _(kind=kind):
                wrap_out(kind).wait_send()

            @pl.when(zl == 1)
            def _(kind=kind):
                wrap_relay(kind).wait_send()

    def wrap_own(kind):
        @pl.when(zl == 0)
        def _():
            wrap_out(kind).start()

    def send_before(kind):
        @pl.when((zl > 0) & (zl < LINE - 1))
        def _():
            kv_copy(kind, 0).start()

    def arrive(kind, s):
        @pl.when(zl > s + 1)
        def _():
            ref = (values if kind else keys).at[zl - 2 - s]
            pltpu.make_async_copy(ref, ref, kvrecv.at[kind * STEPS + s]).wait()

        if s + 1 < STEPS:

            @pl.when((zl > s + 1) & (zl < LINE - 1))
            def _():
                kv_copy(kind, s + 1).start()

    prev_copy = remote(tokens, prev.at[mine], misc.at[8], misc.at[9], at(x, y, z + 1, c))
    prev_share = remote(prev.at[mine], prev.at[mine], misc.at[10], misc.at[11], partner)

    def send_tokens():
        @pl.when(zl < LINE - 1)
        def _():
            prev_copy.start()

    def share_tokens():
        @pl.when(zl > 0)
        def _():
            prev_copy.wait_recv()
            prev_share.start()

    def tokens_before():
        @pl.when(zl > 0)
        def _():
            prev_share.wait_recv()

    def make_keys(rows, slot, first):
        two = jnp.dot(rows[...], W[:, 1024:1280], preferred_element_type=jnp.float32)
        for h in range(2):
            value = rotated(two[:, h * 128 : (h + 1) * 128], first)
            keys[slot, h] = value.astype(jnp.bfloat16)

    def make_values(rows, slot):
        two = jnp.dot(rows[...], W[:, 1280:1536], preferred_element_type=jnp.float32)
        for h in range(2):
            values[slot, h] = two[:, h * 128 : (h + 1) * 128].T.astype(jnp.bfloat16)

    def keys_of_both():
        @pl.when(zl > 0)
        def _():
            make_keys(prev, zl - 1, 0)

        send_before(0)
        make_keys(tok, zl, 256)
        wrap_own(0)

    def values_of_both():
        @pl.when(zl > 0)
        def _():
            make_values(prev, zl - 1)

        send_before(1)
        make_values(tok, zl)
        wrap_own(1)

    def project_queries(offset):
        def pair(i, carry):
            cols = pl.ds(pl.multiple_of(i * 512 + offset * 128, 256), 256)
            two = jnp.dot(tok[...], W[:, cols], preferred_element_type=jnp.float32)
            for j in range(2):
                one = rotated(two[:, j * 128 : (j + 1) * 128], 256)
                q[i * 4 + offset + j] = one.T.astype(jnp.bfloat16)
            return carry

        lax.fori_loop(0, 2, pair, 0)

    def attend(slot, offset, masked):
        def group(i, carry):
            key, value = keys[slot, i], values[slot, i]
            for j in range(2):
                h = i * 4 + offset + j
                s = jnp.dot(key, q[h], preferred_element_type=jnp.float32)
                if masked:
                    row = lax.broadcasted_iota(jnp.int32, (256, 256), 0)
                    column = lax.broadcasted_iota(jnp.int32, (256, 256), 1)
                    s = jnp.where(row <= column, s, -jnp.inf)
                    m = jnp.max(s, axis=0, keepdims=True)
                else:
                    old = top[h]
                    m = jnp.maximum(old, jnp.max(s, axis=0, keepdims=True))
                p = jnp.exp2((s - m) * POWER)
                mass = jnp.sum(p, axis=0, keepdims=True)
                part = jnp.dot(value, p.astype(jnp.bfloat16), preferred_element_type=jnp.float32)
                top[h] = m
                if masked:
                    total[h] = mass
                    acc[h] = part
                else:
                    shrink = jnp.exp2((old - m) * POWER)
                    total[h] = total[h] * shrink + mass
                    acc[h] = acc[h] * shrink + part
            return carry

        lax.fori_loop(0, 2, group, 0)

    def attend_near(offset):
        attend(zl, offset, True)

        @pl.when(zl > 0)
        def _():
            attend(zl - 1, offset, False)

    def attend_steps(offset, steps):
        for s in steps:

            @pl.when(zl > s + 1)
            def _(s=s):
                attend(zl - 2 - s, offset, False)

    spread(True)
    spread(False)
    pass_on(True)
    pass_on(False)
    send_tokens()
    for g in range(4):
        landed(8 + g, 1)
        first_own(g)
    second_own(0, 1)
    first_near(0, 1)
    second_own(2, 3)
    second_near(0, 0, 1)
    first_near(2, 3)
    first_far(0, 1)
    second_near(1, 0, 1)
    second_near(3, 0, 1)
    second_near(0, 2, 3)
    first_far(2, 3)
    landed(0, 2)
    first_own(4)
    landed(4, 2)
    first_own(5)
    second_near(2, 0, 1)
    second_near(1, 2, 3)
    second_near(3, 2, 3)
    second_own(4, 5)
    tok_local.wait()
    tok_copy.wait_recv()
    share_tokens()
    gathered(0, 1)
    tokens_before()
    keys_of_both()
    second_near(2, 2, 3)
    first_near(4, 5)
    gathered(2, 3)
    values_of_both()
    landed(2, 2)
    first_own(6)
    landed(6, 2)
    first_own(7)
    second_near(0, 4, 5)
    first_far(4, 5)
    second_own(6, 7)
    arrive(0, 0)
    second_near(1, 4, 5)
    second_near(3, 4, 5)
    first_near(6, 7)
    arrive(1, 0)
    second_near(2, 4, 5)
    relay(0)
    second_near(0, 6, 7)
    arrive(0, 1)
    relay(1)
    first_far(6, 7)
    gathered(4, 5)
    arrive(1, 1)
    project_queries(0)
    second_near(1, 6, 7)
    second_near(3, 6, 7)
    attend_near(0)
    arrive(0, 2)
    second_near(2, 6, 7)
    attend_steps(0, (0, 1))
    arrive(1, 2)
    gathered(6, 7)
    project_queries(2)
    attend_near(2)
    arrive(0, 3)
    attend_steps(0, (2,))
    attend_steps(2, (0, 1))
    arrive(1, 3)
    attend_steps(2, (2,))
    wrapped(0)
    wrapped(1)
    attend_wrapped(0)
    attend_wrapped(2)
    attend_steps(0, (3,))
    attend_steps(2, (3,))
    arrive(0, 4)
    arrive(1, 4)
    attend_steps(0, (4,))
    attend_steps(2, (4,))

    for h in range(8):
        value = acc[h] * (1.0 / total[h])
        ctx[:, h * 128 : (h + 1) * 128] = value.T.astype(jnp.bfloat16)
    columns = pl.ds(pl.multiple_of(c * 1024, 1024), 1024)
    out_copy = remote(
        ctx.at[theirs], out.at[:, columns], misc.at[6], misc.at[7], partner
    )
    out_copy.start()
    out_local = pltpu.make_async_copy(ctx.at[mine], out.at[:, columns], misc.at[5])
    out_local.start()

    w_copy.wait_send()
    tok_copy.wait_send()

    @pl.when(zl < LINE - 1)
    def _():
        prev_copy.wait_send()

    @pl.when(zl > 0)
    def _():
        prev_share.wait_send()

    spread_done()
    wrap_done()
    for g in range(len(GROUPS)):
        planes_done(g)
    for kind in range(2):
        for s in range(STEPS):

            @pl.when((zl > s) & (zl < LINE - 1))
            def _(kind=kind, s=s):
                kv_copy(kind, s).wait_send()

    out_local.wait()
    out_copy.wait()


def shards(tokens, master, moment_one, moment_two, gradient):
    new_master = adam_step(master, moment_one, moment_two, gradient)
    weights = new_master.astype(jnp.bfloat16)
    half = HEAD_DIM // 2
    frequency = rope_theta ** (-(jnp.arange(half).astype(jnp.float32) * 2.0) / HEAD_DIM)
    chip = lax.div(lax.axis_index("seq"), 2)
    positions = (chip * 256 - 256 + jnp.arange(512)).astype(jnp.float32)
    angles = positions[:, None] * frequency[None, :]
    cosine, sine = jnp.cos(angles), jnp.sin(angles)
    cos = jnp.concatenate([cosine, cosine], axis=1)
    sin = jnp.concatenate([-sine, sine], axis=1)
    vmem = pl.BlockSpec(memory_space=pltpu.VMEM)
    anywhere = pl.BlockSpec(memory_space=pl.ANY)
    bf16, f32 = jnp.bfloat16, jnp.float32
    dma = pltpu.SemaphoreType.DMA
    context = pl.pallas_call(
        kernel,
        name="gather_attend",
        out_shape=jax.ShapeDtypeStruct((128, 2048), bf16),
        in_specs=[anywhere, vmem, vmem, vmem],
        out_specs=anywhere,
        scratch_shapes=[
            pltpu.VMEM((64, 192), bf16),
            pltpu.VMEM((3, 64, 128), bf16),
            pltpu.VMEM((2048, 1536), bf16),
            pltpu.VMEM((256, 2048), bf16),
            pltpu.VMEM((256, 2048), bf16),
            pltpu.VMEM((LINE, 2, 256, 128), bf16),
            pltpu.VMEM((LINE, 2, 128, 256), bf16),
            pltpu.VMEM((8, 128, 256), bf16),
            pltpu.VMEM((8, 128, 256), f32),
            pltpu.VMEM((8, 1, 256), f32),
            pltpu.VMEM((8, 1, 256), f32),
            pltpu.VMEM((256, 1024), bf16),
            pltpu.VMEM((2, 256, 128), bf16),
            pltpu.VMEM((2, 128, 256), bf16),
            dma((12,)), dma((3,)), dma((9,)), dma((24,)), dma((8,)), dma((32,)), dma((8,)),
            dma((128,)), dma((2 * STEPS,)), dma((2 * STEPS,)), dma((4,)), dma((4,)),
        ],
        compiler_params=pltpu.CompilerParams(
            collective_id=0, has_side_effects=True, vmem_limit_bytes=48 * 1024 * 1024
        ),
    )(tokens[0], weights, cos, sin)
    return context[None], new_master


def solution(mesh):
    placed = (P("dp", "seq", None), P("dp", "seq"), P("dp", "seq"), P("dp", "seq"), P("dp", "seq"))
    return jax.shard_map(
        shards,
        mesh=mesh,
        in_specs=placed,
        out_specs=(P("dp", "seq", None), P("dp", "seq")),
        check_vma=False,
    )
```

```python
import functools
import math

import jax
import jax.numpy as jnp
from jax import lax
from jax.experimental import pallas as pl
from jax.experimental.pallas import tpu as pltpu
from jax.sharding import PartitionSpec as P

HEADS = 16
KV_HEADS = 4
HEAD_DIM = 128
SIDE = 4
LINE = 8
RING = 16
MESH = pl.DeviceIdType.MESH

beta_one = 0.9
beta_two = 0.999
learn_rate = 0.005
decay_rate = 0.1
adam_eps = 1e-08
rope_theta = 500000.0
correct_one = 1.0 - math.exp(1000.0 * math.log(beta_one))
correct_two = 1.0 - math.exp(1000.0 * math.log(beta_two))

SCALE = 1.0 / math.sqrt(HEAD_DIM)
BLK = 128
SUB = 64
ROWS = 128
GROUPS = (
    (1024, 128, True), (1152, 128, False), (1280, 128, True), (1408, 128, False),
    (0, 256, True), (512, 256, False), (256, 256, True), (768, 256, False),
)
COARSE = (8, 4, 12)
STEPS = 5
POWER = SCALE / math.log(2.0)


def adam_step(master, moment_one, moment_two, gradient):
    first = beta_one * moment_one + (1.0 - beta_one) * gradient
    second = beta_two * moment_two + (1.0 - beta_two) * gradient * gradient
    update = first / correct_one / (jnp.sqrt(second / correct_two) + adam_eps)
    return master - learn_rate * (update + decay_rate * master)


def kernel(
    tokens, shard, cos, sin, out,
    other, blk, W, tok, prev, keys, values, q, acc, top, total, ctx,
    far_keys, far_values, misc, zsend, zpass, zrecv, s1send, s1recv, s2send, s2recv, kvsend, kvrecv, wrapsend, wraprecv,
):
    dp, seq = lax.axis_index("dp"), lax.axis_index("seq")
    zh = lax.rem(dp, 2)
    xy = lax.div(dp, 2)
    x, y = lax.div(xy, SIDE), lax.rem(xy, SIDE)
    c = lax.rem(seq, 2)
    zl = lax.div(seq, 2)
    z = zh * LINE + zl

    def at(xx, yy, zz, cc):
        return {
            "dp": (xx * SIDE + yy) * 2 + lax.div(zz, LINE),
            "seq": lax.rem(zz, LINE) * 2 + cc,
        }

    def xat(d):
        return lax.rem(x + (SIDE + d) % SIDE, SIDE)

    def yat(d):
        return lax.rem(y + (SIDE + d) % SIDE, SIDE)

    partner = at(x, y, z, 1 - c)

    barrier = pltpu.get_barrier_semaphore()

    def greet(target):
        pl.semaphore_signal(barrier, inc=1, device_id=target, device_id_type=MESH)

    greet(partner)
    for d in range(1, SIDE):
        greet(at(xat(d), y, z, c))
        greet(at(x, yat(d), z, c))

    def greet_z(d, carry):
        greet(at(x, y, lax.rem(z + d, RING), c))
        return carry

    lax.fori_loop(1, RING, greet_z, 0)
    mine = pl.ds(pl.multiple_of(c * 128, 128), 128)
    theirs = pl.ds(pl.multiple_of((1 - c) * 128, 128), 128)
    tok_local = pltpu.make_async_copy(tokens, tok.at[mine], misc.at[0])
    tok_local.start()
    pl.semaphore_wait(barrier, 1 + 2 * (SIDE - 1) + RING - 1)

    def remote(src, dst, send, recv, target):
        return pltpu.make_async_remote_copy(
            src_ref=src, dst_ref=dst, send_sem=send, recv_sem=recv,
            device_id=target, device_id_type=MESH,
        )

    w_copy = remote(shard, other, misc.at[3], misc.at[4], partner)
    w_copy.start()
    tok_copy = remote(tokens, tok.at[mine], misc.at[1], misc.at[2], partner)
    tok_copy.start()
    w_copy.wait_recv()

    own_shard = shard[...].astype(jnp.float32)
    other_shard = other[...].astype(jnp.float32)
    low = jnp.where(c == 0, own_shard, other_shard)
    high = jnp.where(c == 0, other_shard, own_shard)
    blk[0] = low[:, :128].astype(jnp.bfloat16)
    blk[1] = jnp.concatenate([low[:, 128:], high[:, :64]], axis=1).astype(jnp.bfloat16)
    blk[2] = high[:, 64:].astype(jnp.bfloat16)

    def place(zhalf, column):
        rows = pl.ds(pl.multiple_of(xy * ROWS + zhalf * SUB, SUB), SUB)
        return W.at[rows, pl.ds(pl.multiple_of(column, BLK), BLK)]

    def block_of(line, j, keys_or_values):
        b = line * 3 + j
        past = b - HEADS
        if keys_or_values:
            local = 8 + lax.div(past, KV_HEADS) * 2 + lax.rem(past, 2)
            return local, (b >= HEADS) & (lax.rem(lax.div(past, 2), 2) == c)
        return lax.rem(b, 8), (b < HEADS) & (lax.div(b, 8) == c)

    fine = (1, RING - 1, 2 + 12 * c)

    def z_send(src, where, send, recv, steps):
        for d in steps:
            remote(src, where, send, recv, at(x, y, lax.rem(z + d, RING), c)).start()

    def spread(kind):
        for j in range(3):
            local, wanted = block_of(zl, j, kind)

            @pl.when(wanted)
            def _(j=j, local=local):
                where = place(zh, local * BLK)
                sem = zrecv.at[local * 2 + zh]
                z_send(blk.at[j], where, zsend.at[j], sem, COARSE + fine)
                pltpu.make_async_copy(blk.at[j], where, sem).start()

    def pass_on(kind):
        for i, d in enumerate(COARSE):
            source = lax.rem(z + RING - d, RING)
            half = lax.div(source, LINE)
            for j in range(3):
                local, wanted = block_of(lax.rem(source, LINE), j, kind)

                @pl.when(wanted)
                def _(i=i, j=j, local=local, half=half):
                    where = place(half, local * BLK)
                    sem = zrecv.at[local * 2 + half]
                    pltpu.make_async_copy(where, where, sem).wait()
                    z_send(where, where, zpass.at[i * 3 + j], sem, fine)

    def spread_done():
        for kind in (True, False):
            for j in range(3):
                _, wanted = block_of(zl, j, kind)

                @pl.when(wanted)
                def _(j=j):
                    ref = W.at[pl.ds(0, SUB * 6), pl.ds(0, BLK)]
                    pltpu.make_async_copy(ref, ref, zsend.at[j]).wait()

                for i, d in enumerate(COARSE):
                    _, passed = block_of(lax.rem(z + RING - d, LINE), j, kind)

                    @pl.when(passed)
                    def _(i=i, j=j):
                        ref = W.at[pl.ds(0, SUB * 3), pl.ds(0, BLK)]
                        pltpu.make_async_copy(ref, ref, zpass.at[i * 3 + j]).wait()

    def landed(first, count):
        for local in range(first, first + count):
            if local < 8:
                b = c * 8 + local
            elif local < 10:
                b = HEADS + c * 2 + local - 8
            else:
                b = HEADS + KV_HEADS + c * 2 + local - 10
            for half in range(2):
                steps = lax.rem(z + RING - (lax.div(b, 3) + half * LINE), RING)

                @pl.when((lax.rem(steps, 4) != 0) | (steps == 0))
                def _(local=local, half=half):
                    ref = place(half, local * BLK)
                    pltpu.make_async_copy(ref, ref, zrecv.at[local * 2 + half]).wait()

    def ring(g, stage, d):
        along_x = GROUPS[g][2] == (stage == 1)

        def ref(step, first=0, count=ROWS):
            dx, dy = (-step, -d) if along_x else (-d, -step)
            rows = pl.multiple_of((xat(dx) * SIDE + yat(dy)) * ROWS + first, SUB)
            return W.at[pl.ds(rows, count), pl.ds(GROUPS[g][0], GROUPS[g][1])]

        up = at(xat(1), y, z, c) if along_x else at(x, yat(1), z, c)
        down = at(xat(-1), y, z, c) if along_x else at(x, yat(-1), z, c)
        if stage == 1:
            return ref, up, down, s1send.at[g], lambda i: s1recv.at[g * 4 + i]
        return ref, up, down, s2send.at[g], lambda i: s2recv.at[(g * 4 + d) * 4 + i]

    def begin(g, stage, d=0):
        ref, up, down, send, recv = ring(g, stage, d)
        remote(ref(0), ref(0), send, recv(0), up).start()
        remote(ref(0), ref(0), send, recv(1), down).start()

    def hand_on(g, stage, d=0):
        ref, up, down, send, recv = ring(g, stage, d)
        pltpu.make_async_copy(ref(1), ref(1), recv(0)).wait()
        half = ref(1, 0, SUB)
        remote(half, half, send, recv(2), up).start()
        pltpu.make_async_copy(ref(3), ref(3), recv(1)).wait()
        half = ref(3, SUB, SUB)
        remote(half, half, send, recv(3), down).start()

    def complete(g, stage, d=0):
        ref, _, _, _, recv = ring(g, stage, d)
        for i in range(2):
            half = ref(2, i * SUB, SUB)
            pltpu.make_async_copy(half, half, recv(2 + i)).wait()

    def first_own(*groups):
        for g in groups:
            begin(g, 1)

    def second_own(*groups):
        for g in groups:
            begin(g, 2, 0)

    def first_near(*groups):
        for g in groups:
            hand_on(g, 1)
            begin(g, 2, 1)
            begin(g, 2, 3)

    def first_far(*groups):
        for g in groups:
            complete(g, 1)
            begin(g, 2, 2)

    def second_near(d, *groups):
        for g in groups:
            hand_on(g, 2, d)

    def gathered(*groups):
        for g in groups:
            for d in (0, 1, 3, 2):
                complete(g, 2, d)

    def planes_done(g):
        first, width, _ = GROUPS[g]
        ref = W.at[pl.ds(0, 3 * ROWS), pl.ds(first, width)]
        pltpu.make_async_copy(ref, ref, s1send.at[g]).wait()
        ref = W.at[pl.ds(0, 12 * ROWS), pl.ds(first, width)]
        pltpu.make_async_copy(ref, ref, s2send.at[g]).wait()

    def rotated(value, first):
        rows = slice(first, first + 256)
        return value * cos[rows] + pltpu.roll(value, 64, 1) * sin[rows]

    def kv_copy(kind, s):
        ref = (values if kind else keys).at[zl - 1 - s]
        sem = kind * STEPS + s
        return remote(ref, ref, kvsend.at[sem], kvrecv.at[sem], at(x, y, z + 1, c))

    def wrap_out(kind):
        return remote(
            (values if kind else keys).at[0], far_values if kind else far_keys,
            wrapsend.at[kind], wraprecv.at[kind], at(x, y, lax.rem(z + 9, RING), c),
        )

    def wrap_relay(kind):
        return remote(
            far_values if kind else far_keys, (values if kind else keys).at[0],
            wrapsend.at[2 + kind], wraprecv.at[2 + kind], at(x, y, lax.rem(z + RING - 2, RING), c),
        )

    def relay(kind):
        @pl.when(zl == 1)
        def _():
            ref = far_values if kind else far_keys
            pltpu.make_async_copy(ref, ref, wraprecv.at[kind]).wait()
            wrap_relay(kind).start()

    def wrapped(kind):
        @pl.when(zl == LINE - 1)
        def _():
            ref = (values if kind else keys).at[0]
            pltpu.make_async_copy(ref, ref, wraprecv.at[2 + kind]).wait()

    def wrap_done():
        for kind in range(2):

            @pl.when(zl == 0)
            def _(kind=kind):
                wrap_out(kind).wait_send()

            @pl.when(zl == 1)
            def _(kind=kind):
                wrap_relay(kind).wait_send()

    def wrap_own(kind):
        @pl.when(zl == 0)
        def _():
            wrap_out(kind).start()

    def send_before(kind):
        @pl.when((zl > 0) & (zl < LINE - 1))
        def _():
            kv_copy(kind, 0).start()

    def arrive(kind, s):
        @pl.when(zl > s + 1)
        def _():
            ref = (values if kind else keys).at[zl - 2 - s]
            pltpu.make_async_copy(ref, ref, kvrecv.at[kind * STEPS + s]).wait()

        if s + 1 < STEPS:

            @pl.when((zl > s + 1) & (zl < LINE - 1))
            def _():
                kv_copy(kind, s + 1).start()

    prev_copy = remote(tokens, prev.at[mine], misc.at[8], misc.at[9], at(x, y, z + 1, c))
    prev_share = remote(prev.at[mine], prev.at[mine], misc.at[10], misc.at[11], partner)

    def send_tokens():
        @pl.when(zl < LINE - 1)
        def _():
            prev_copy.start()

    def share_tokens():
        @pl.when(zl > 0)
        def _():
            prev_copy.wait_recv()
            prev_share.start()

    def tokens_before():
        @pl.when(zl > 0)
        def _():
            prev_share.wait_recv()

    def make_keys(rows, slot, first):
        two = jnp.dot(rows[...], W[:, 1024:1280], preferred_element_type=jnp.float32)
        for h in range(2):
            value = rotated(two[:, h * 128 : (h + 1) * 128], first)
            keys[slot, h] = value.astype(jnp.bfloat16)

    def make_values(rows, slot):
        two = jnp.dot(rows[...], W[:, 1280:1536], preferred_element_type=jnp.float32)
        for h in range(2):
            values[slot, h] = two[:, h * 128 : (h + 1) * 128].T.astype(jnp.bfloat16)

    def keys_of_both():
        @pl.when(zl > 0)
        def _():
            make_keys(prev, zl - 1, 0)

        send_before(0)
        make_keys(tok, zl, 256)
        wrap_own(0)

    def values_of_both():
        @pl.when(zl > 0)
        def _():
            make_values(prev, zl - 1)

        send_before(1)
        make_values(tok, zl)
        wrap_own(1)

    def project_queries(offset):
        def pair(i, carry):
            cols = pl.ds(pl.multiple_of(i * 512 + offset * 128, 256), 256)
            two = jnp.dot(tok[...], W[:, cols], preferred_element_type=jnp.float32)
            for j in range(2):
                one = rotated(two[:, j * 128 : (j + 1) * 128], 256)
                q[i * 4 + offset + j] = one.T.astype(jnp.bfloat16)
            return carry

        lax.fori_loop(0, 2, pair, 0)

    def attend(slot, offset, masked):
        def group(i, carry):
            key, value = keys[slot, i], values[slot, i]
            for j in range(2):
                h = i * 4 + offset + j
                s = jnp.dot(key, q[h], preferred_element_type=jnp.float32)
                if masked:
                    row = lax.broadcasted_iota(jnp.int32, (256, 256), 0)
                    column = lax.broadcasted_iota(jnp.int32, (256, 256), 1)
                    s = jnp.where(row <= column, s, -jnp.inf)
                    m = jnp.max(s, axis=0, keepdims=True)
                else:
                    old = top[h]
                    m = jnp.maximum(old, jnp.max(s, axis=0, keepdims=True))
                p = jnp.exp2((s - m) * POWER)
                mass = jnp.sum(p, axis=0, keepdims=True)
                part = jnp.dot(value, p.astype(jnp.bfloat16), preferred_element_type=jnp.float32)
                top[h] = m
                if masked:
                    total[h] = mass
                    acc[h] = part
                else:
                    shrink = jnp.exp2((old - m) * POWER)
                    total[h] = total[h] * shrink + mass
                    acc[h] = acc[h] * shrink + part
            return carry

        lax.fori_loop(0, 2, group, 0)

    def attend_many(slots, offset, first=False):
        def group(i, carry):
            for j in range(2):
                h = i * 4 + offset + j
                scores = [
                    jnp.dot(keys[t, i], q[h], preferred_element_type=jnp.float32) for t in slots
                ]
                if first:
                    row = lax.broadcasted_iota(jnp.int32, (256, 256), 0)
                    column = lax.broadcasted_iota(jnp.int32, (256, 256), 1)
                    scores[0] = jnp.where(row <= column, scores[0], -jnp.inf)
                m = functools.reduce(jnp.maximum, scores)
                m = jnp.max(m, axis=0, keepdims=True)
                if not first:
                    old = top[h]
                    m = jnp.maximum(old, m)
                parts = [jnp.exp2((one - m) * POWER) for one in scores]
                mass = jnp.sum(functools.reduce(jnp.add, parts), axis=0, keepdims=True)
                top[h] = m
                if not first:
                    shrink = jnp.exp2((old - m) * POWER)
                    mass = mass + total[h] * shrink
                total[h] = mass
                result = None if first else acc[h] * shrink
                for t, one in zip(slots, parts):
                    part = jnp.dot(
                        values[t, i], one.astype(jnp.bfloat16), preferred_element_type=jnp.float32
                    )
                    result = part if result is None else result + part
                acc[h] = result
            return carry

        lax.fori_loop(0, 2, group, 0)

    def attend_near(offset):
        @pl.when(zl == 0)
        def _():
            attend(zl, offset, True)

        @pl.when(zl > 0)
        def _():
            attend_many((zl, zl - 1), offset, True)

    def attend_run(offset, steps):
        @pl.when(zl > steps[-1] + 1)
        def _():
            attend_many([zl - 2 - s for s in steps], offset)

        for s in steps[:-1]:

            @pl.when((zl > s + 1) & (zl <= steps[-1] + 1))
            def _(s=s):
                attend(zl - 2 - s, offset, False)

    def attend_last(offset):
        @pl.when(zl == LINE - 2)
        def _():
            attend(0, offset, False)

        @pl.when(zl == LINE - 1)
        def _():
            attend_many((1, 0), offset)

    spread(True)
    spread(False)
    pass_on(True)
    pass_on(False)
    send_tokens()
    for g in range(4):
        landed(8 + g, 1)
        first_own(g)
    second_own(0, 1)
    first_near(0, 1)
    second_own(2, 3)
    second_near(0, 0, 1)
    first_near(2, 3)
    first_far(0, 1)
    second_near(1, 0, 1)
    second_near(3, 0, 1)
    second_near(0, 2, 3)
    first_far(2, 3)
    landed(0, 2)
    first_own(4)
    landed(4, 2)
    first_own(5)
    second_near(2, 0, 1)
    second_near(1, 2, 3)
    second_near(3, 2, 3)
    second_own(4, 5)
    tok_local.wait()
    tok_copy.wait_recv()
    share_tokens()
    gathered(0, 1)
    tokens_before()
    keys_of_both()
    second_near(2, 2, 3)
    first_near(4, 5)
    gathered(2, 3)
    values_of_both()
    landed(2, 2)
    first_own(6)
    landed(6, 2)
    first_own(7)
    second_near(0, 4, 5)
    first_far(4, 5)
    second_own(6, 7)
    arrive(0, 0)
    second_near(1, 4, 5)
    second_near(3, 4, 5)
    first_near(6, 7)
    arrive(1, 0)
    second_near(2, 4, 5)
    relay(0)
    second_near(0, 6, 7)
    arrive(0, 1)
    relay(1)
    first_far(6, 7)
    gathered(4, 5)
    arrive(1, 1)
    project_queries(0)
    second_near(1, 6, 7)
    second_near(3, 6, 7)
    attend_near(0)
    arrive(0, 2)
    second_near(2, 6, 7)
    attend_run(0, (0, 1))
    arrive(1, 2)
    gathered(6, 7)
    project_queries(2)
    attend_near(2)
    arrive(0, 3)
    arrive(1, 3)
    attend_run(0, (2, 3))
    attend_run(2, (0, 1, 2, 3))
    wrapped(0)
    wrapped(1)
    arrive(0, 4)
    arrive(1, 4)
    attend_last(0)
    attend_last(2)

    for h in range(8):
        value = acc[h] * (1.0 / total[h])
        ctx[:, h * 128 : (h + 1) * 128] = value.T.astype(jnp.bfloat16)
    columns = pl.ds(pl.multiple_of(c * 1024, 1024), 1024)
    out_copy = remote(
        ctx.at[theirs], out.at[:, columns], misc.at[6], misc.at[7], partner
    )
    out_copy.start()
    out_local = pltpu.make_async_copy(ctx.at[mine], out.at[:, columns], misc.at[5])
    out_local.start()

    w_copy.wait_send()
    tok_copy.wait_send()

    @pl.when(zl < LINE - 1)
    def _():
        prev_copy.wait_send()

    @pl.when(zl > 0)
    def _():
        prev_share.wait_send()

    spread_done()
    wrap_done()
    for g in range(len(GROUPS)):
        planes_done(g)
    for kind in range(2):
        for s in range(STEPS):

            @pl.when((zl > s) & (zl < LINE - 1))
            def _(kind=kind, s=s):
                kv_copy(kind, s).wait_send()

    out_local.wait()
    out_copy.wait()


def shards(tokens, master, moment_one, moment_two, gradient):
    new_master = adam_step(master, moment_one, moment_two, gradient)
    weights = new_master.astype(jnp.bfloat16)
    half = HEAD_DIM // 2
    frequency = rope_theta ** (-(jnp.arange(half).astype(jnp.float32) * 2.0) / HEAD_DIM)
    chip = lax.div(lax.axis_index("seq"), 2)
    positions = (chip * 256 - 256 + jnp.arange(512)).astype(jnp.float32)
    angles = positions[:, None] * frequency[None, :]
    cosine, sine = jnp.cos(angles), jnp.sin(angles)
    cos = jnp.concatenate([cosine, cosine], axis=1)
    sin = jnp.concatenate([-sine, sine], axis=1)
    vmem = pl.BlockSpec(memory_space=pltpu.VMEM)
    anywhere = pl.BlockSpec(memory_space=pl.ANY)
    bf16, f32 = jnp.bfloat16, jnp.float32
    dma = pltpu.SemaphoreType.DMA
    context = pl.pallas_call(
        kernel,
        name="gather_attend",
        out_shape=jax.ShapeDtypeStruct((128, 2048), bf16),
        in_specs=[anywhere, vmem, vmem, vmem],
        out_specs=anywhere,
        scratch_shapes=[
            pltpu.VMEM((64, 192), bf16),
            pltpu.VMEM((3, 64, 128), bf16),
            pltpu.VMEM((2048, 1536), bf16),
            pltpu.VMEM((256, 2048), bf16),
            pltpu.VMEM((256, 2048), bf16),
            pltpu.VMEM((LINE, 2, 256, 128), bf16),
            pltpu.VMEM((LINE, 2, 128, 256), bf16),
            pltpu.VMEM((8, 128, 256), bf16),
            pltpu.VMEM((8, 128, 256), f32),
            pltpu.VMEM((8, 1, 256), f32),
            pltpu.VMEM((8, 1, 256), f32),
            pltpu.VMEM((256, 1024), bf16),
            pltpu.VMEM((2, 256, 128), bf16),
            pltpu.VMEM((2, 128, 256), bf16),
            dma((12,)), dma((3,)), dma((9,)), dma((24,)), dma((8,)), dma((32,)), dma((8,)),
            dma((128,)), dma((2 * STEPS,)), dma((2 * STEPS,)), dma((4,)), dma((4,)),
        ],
        compiler_params=pltpu.CompilerParams(
            collective_id=0, has_side_effects=True, vmem_limit_bytes=48 * 1024 * 1024
        ),
    )(tokens[0], weights, cos, sin)
    return context[None], new_master


def solution(mesh):
    placed = (P("dp", "seq", None), P("dp", "seq"), P("dp", "seq"), P("dp", "seq"), P("dp", "seq"))
    return jax.shard_map(
        shards,
        mesh=mesh,
        in_specs=placed,
        out_specs=(P("dp", "seq", None), P("dp", "seq")),
        check_vma=False,
    )
```
